32 devices in a mesh: gz: 16 (over z, x, core), gy: 2 (over y).
Axes of the slice: x: 2, y: 2, z: 4, core: 2. Of those that a mesh axis runs over, the one named last changes fastest.
Arguments:
- spread_weights: float32 [64, 32768], P(None, ('gz', 'gy')), may hold values from -6 to 6
- spread_base: int32 [3, 32768], P(None, ('gz', 'gy')), may hold values from 0 to 383, as said below
- qm_base: int32 [3, 4096], P(None, ('gz', 'gy')), may hold values from 0 to 383, as said below
- qm_frac: float32 [3, 4096], P(None, ('gz', 'gy')), may hold values from 0 to 1
- qm_charge: float32 [4096], P(('gz', 'gy')), may hold values from -3 to 3
Outputs:
- qm_forces: float32 [3, 4096], P(None, ('gz', 'gy'))
The draws below stay inside these ranges and needn't reach their ends.
Inputs may be any that keep to these rules, and one draw needn't show every extreme that they name: For point charge j let d = j // 1024, p = d // 2 and q = d % 2; then spread_base[0, j] lies in [p * 24, (p + 1) * 24) and spread_base[1, j] in [q * 192, (q + 1) * 192); spread_base[2, j] is any cell. For quantum-region atom i let d = i // 128, p = d // 2 and q = d % 2; then qm_base[0, i] lies in [p * 24, (p + 1) * 24) and qm_base[1, i] in [q * 192, (q + 1) * 192); qm_base[2, i] is any cell.
All inputs are finite; a program needn't handle non-finite values.
Results may differ from the reference program's by a relative error of at most 0.0003.
Values sent between devices are 32-bit elements; how exact they have to be, the bound alone decides.
A program may use at most 256 MiB of HBM per device.

```python
import math
import jax
import jax.numpy as jnp

GRID = 384
ORDER = 4
ATOMS_DEV = 1024
QM_DEV = 128
ZLOC = 24
YLOC = 192
ATOMS = 32768
QMS = 4096


def place_bases(key, total, per_device):
    index = jnp.arange(total, dtype=jnp.int32)
    device = index // per_device
    groups = GRID // YLOC
    z_part = device // groups
    y_part = device % groups
    key_z, key_y, key_x = jax.random.split(key, 3)
    first_z = z_part * ZLOC + jax.random.randint(key_z, (total,), 0, ZLOC, dtype=jnp.int32)
    first_y = y_part * YLOC + jax.random.randint(key_y, (total,), 0, YLOC, dtype=jnp.int32)
    first_x = jax.random.randint(key_x, (total,), 0, GRID, dtype=jnp.int32)
    return jnp.stack([first_z, first_y, first_x]).astype(jnp.int32)


def draw_spread_base(key, part):
    return place_bases(jax.random.fold_in(key, 11), ATOMS, ATOMS_DEV)


def draw_qm_base(key, part):
    return place_bases(jax.random.fold_in(key, 23), QMS, QM_DEV)


def block_scale(own_key, extent, cuts, low, top_value):
    loudness, own = 1.0, jax.random.fold_in(own_key, 6)
    for position, blocks in cuts:
        draws = jnp.exp(jax.random.uniform(jax.random.fold_in(own, position), (blocks,), jnp.float32, low / len(cuts), top_value / len(cuts)))
        loudness = loudness * jnp.repeat(draws, extent[position] // blocks).reshape([-1 if axis == position else 1 for axis in range(len(extent))])
    return loudness


def normal_values(rng, shape, deviation, limit, shards=(), kind=jnp.bfloat16):
    drawn = jax.random.normal(rng, shape, jnp.float32) * deviation
    if len(shards) > 0:
        drawn = block_scale(rng, shape, shards, -0.22, 0.18) * drawn
    return jnp.clip(drawn, min=-limit, max=limit).astype(kind)


def setup_inputs(seed: int = 0) -> dict:
    keys = jax.random.split(jax.random.key(seed), 6)
    return {
        "spread_weights": normal_values(keys[0], (ORDER * ORDER * ORDER, ATOMS), 1.0, 6.0, ((1, 32),), jnp.float32),
        "spread_base": draw_spread_base(jax.random.fold_in(keys[5], 71), 0),
        "qm_base": draw_qm_base(jax.random.fold_in(keys[5], 71), 0),
        "qm_frac": jnp.clip(1.0 * jax.random.uniform(keys[3], (3, QMS), jnp.float32) ** block_scale(keys[3], (3, QMS), ((1, 32),), -0.2, 0.2), 0.0, 1.0),
        "qm_charge": normal_values(keys[4], (QMS,), 0.5, 3.0, ((0, 32),), jnp.float32),
    }


SPLITTING = 0.8


def moduli(index, points):
    signed = jnp.where(index < points // 2, index, index - points).astype(jnp.float32) / points
    spline = 2.0 / 3.0 + jnp.cos((2.0 * math.pi / points) * index.astype(jnp.float32)) / 3.0
    return signed * signed, 1.0 / (spline * spline), index == points // 2


def influence(first, second, third, points):
    sq_one, mod_one, edge_one = moduli(first, points)
    sq_two, mod_two, edge_two = moduli(second, points)
    sq_three, mod_three, edge_three = moduli(third, points)
    total = sq_one + sq_two + sq_three
    safe = jnp.where(total > 0.0, total, 1.0)
    value = mod_one * mod_two * mod_three * jnp.exp(-(math.pi * math.pi / (SPLITTING * SPLITTING)) * total) / (math.pi * safe)
    keep = (total > 0.0) & jnp.logical_not(edge_one | edge_two | edge_three)
    return jnp.where(keep, value, 0.0)


def spline_weights(frac):
    remain = 1.0 - frac
    square = frac * frac
    cubed = square * frac
    values = jnp.stack([remain * remain * remain / 6.0, (3.0 * cubed - 6.0 * square + 4.0) / 6.0,
                        (-3.0 * cubed + 3.0 * square + 3.0 * frac + 1.0) / 6.0, cubed / 6.0])
    slopes = jnp.stack([-0.5 * remain * remain, (3.0 * square - 4.0 * frac) / 2.0,
                        (-3.0 * square + 2.0 * frac + 1.0) / 2.0, 0.5 * square])
    return values, slopes


def forces_from(patch, qm_frac, qm_charge):
    w_z, d_z = spline_weights(qm_frac[0])
    w_y, d_y = spline_weights(qm_frac[1])
    w_x, d_x = spline_weights(qm_frac[2])

    def contract(first, second, third):
        return jnp.sum(patch * (first[:, None, None, :] * second[None, :, None, :] * third[None, None, :, :]), axis=(0, 1, 2))

    return jnp.stack([-qm_charge * contract(d_z, w_y, w_x), -qm_charge * contract(w_z, d_y, w_x),
                      -qm_charge * contract(w_z, w_y, d_x)])


def reference(spread_weights, spread_base, qm_base, qm_frac, qm_charge):
    points = GRID
    offsets = jnp.arange(ORDER * ORDER * ORDER, dtype=jnp.int32)
    off_z = offsets // (ORDER * ORDER)
    off_y = (offsets // ORDER) % ORDER
    off_x = offsets % ORDER
    flat_index = (((spread_base[0][None, :] + off_z[:, None]) % points) * points
                  + (spread_base[1][None, :] + off_y[:, None]) % points) * points + (spread_base[2][None, :] + off_x[:, None]) % points
    charge = jnp.zeros((points * points * points,), jnp.float32).at[flat_index.reshape(-1)].add(spread_weights.reshape(-1))
    charge = charge.reshape(points, points, points)
    spectrum = jnp.fft.fftn(charge)
    index = jnp.arange(points, dtype=jnp.int32)
    green = influence(index[:, None, None], index[None, :, None], index[None, None, :], points)
    potential = jnp.real(jnp.fft.ifftn(spectrum * green)).astype(jnp.float32)
    shifts_up = jnp.arange(ORDER, dtype=jnp.int32)[:, None]
    cell_z = (qm_base[0][None, :] + shifts_up) % points
    cell_y = (qm_base[1][None, :] + shifts_up) % points
    cell_x = (qm_base[2][None, :] + shifts_up) % points
    patch = potential[cell_z[:, None, None, :], cell_y[None, :, None, :], cell_x[None, None, :, :]]
    return forces_from(patch, qm_frac, qm_charge)
```

```python
import math

import jax
import jax.numpy as jnp
from jax import lax
from jax.experimental import pallas as pl
from jax.experimental.pallas import tpu as pltpu
from jax.sharding import PartitionSpec as P

GRID = 384
ORDER = 4


SPLITTING = 0.8
HIGHEST = lax.Precision.HIGHEST
HIGH = lax.Precision.HIGH
GROUP = 64


def moduli(index, points):
    signed = jnp.where(index < points // 2, index, index - points).astype(jnp.float32) / points
    spline = 2.0 / 3.0 + jnp.cos(2.0 * math.pi / points * index.astype(jnp.float32)) / 3.0
    return (signed * signed, 1.0 / (spline * spline), index == points // 2)


def influence(first, second, third, points):
    sq_one, mod_one, edge_one = moduli(first, points)
    sq_two, mod_two, edge_two = moduli(second, points)
    sq_three, mod_three, edge_three = moduli(third, points)
    total = sq_one + sq_two + sq_three
    safe = jnp.where(total > 0.0, total, 1.0)
    value = (
        mod_one
        * mod_two
        * mod_three
        * jnp.exp(-(math.pi * math.pi / (SPLITTING * SPLITTING)) * total)
        / (math.pi * safe)
    )
    keep = (total > 0.0) & jnp.logical_not(edge_one | edge_two | edge_three)
    return jnp.where(keep, value, 0.0)


def spline_weights(frac):
    remain = 1.0 - frac
    square = frac * frac
    cubed = square * frac
    values = jnp.stack(
        [
            remain * remain * remain / 6.0,
            (3.0 * cubed - 6.0 * square + 4.0) / 6.0,
            (-3.0 * cubed + 3.0 * square + 3.0 * frac + 1.0) / 6.0,
            cubed / 6.0,
        ]
    )
    slopes = jnp.stack(
        [
            -0.5 * remain * remain,
            (3.0 * square - 4.0 * frac) / 2.0,
            (-3.0 * square + 2.0 * frac + 1.0) / 2.0,
            0.5 * square,
        ]
    )
    return (values, slopes)


def angle_tables(rows_in, cols_in, points):
    product = rows_in[:, None] * cols_in[None, :] % points
    angle = 2.0 * math.pi / points * product.astype(jnp.float32)
    return (jnp.cos(angle), jnp.sin(angle))


def line_tables(cells, values, slopes, extent):
    hits = (jnp.arange(extent, dtype=jnp.int32)[None, :, None] == cells[:, None, :]).astype(
        jnp.float32
    )
    return (jnp.sum(hits * values[:, None, :], axis=0), jnp.sum(hits * slopes[:, None, :], axis=0))


def spread_kernel(first_ref, count_ref, weights_ref, z_ref, y_ref, waves_ref, out_ref):
    half = pl.program_id(0)
    group = pl.program_id(1)

    @pl.when(group == 0)
    def _():
        out_ref[...] = jnp.zeros_like(out_ref)

    rows = out_ref.shape[1]
    weights = weights_ref[...]
    z_cell = z_ref[...]
    y_cell = y_ref[...]
    waves = waves_ref[...]
    high = waves.astype(jnp.bfloat16)
    low = (waves - high.astype(jnp.float32)).astype(jnp.bfloat16)
    first = first_ref[half, group]
    row_offset = lax.broadcasted_iota(jnp.int32, (rows, weights.shape[1]), 0) - y_cell

    def plane(step, carry):
        z = first + step
        offset = z - z_cell
        chosen = jnp.zeros((ORDER, weights.shape[1]), jnp.float32)
        for a in range(ORDER):
            chosen = jnp.where(offset == a, weights[a * ORDER : (a + 1) * ORDER], chosen)
        placed = jnp.zeros((rows, weights.shape[1]), jnp.float32)
        for b in range(ORDER):
            placed = jnp.where(row_offset == b, chosen[b : b + 1], placed)
        top = placed.astype(jnp.bfloat16)
        rest = (placed - top.astype(jnp.float32)).astype(jnp.bfloat16)
        total = jnp.dot(top, high, preferred_element_type=jnp.float32)
        total += jnp.dot(rest, high, preferred_element_type=jnp.float32)
        total += jnp.dot(top, low, preferred_element_type=jnp.float32)
        out_ref[z] += total
        return carry

    lax.fori_loop(0, count_ref[half, group], plane, 0)


def sort_by_plane(table, local_z):
    count = local_z.shape[0]
    order = jnp.arange(count, dtype=jnp.int32)
    before = (local_z[:, None] < local_z[None, :]) | (
        (local_z[:, None] == local_z[None, :]) & (order[:, None] < order[None, :])
    )
    rank = jnp.sum(before.astype(jnp.int32), axis=0)
    moves = (rank[:, None] == order[None, :]).astype(jnp.float32)
    return jnp.dot(table, moves, precision=HIGHEST)


def phases(cells, index, points):
    angle = (2.0 * math.pi / points) * (cells[..., None] * index % points).astype(jnp.float32)
    return (jnp.cos(angle), jnp.sin(angle))


def spread_lines(spread_weights, spread_base, z_first, y_first, z_extent, y_local, kx_index, points):
    count = spread_weights.shape[1]
    halves = lax.axis_size("gy")
    local = jnp.stack([spread_base[0] - z_first, spread_base[1] - y_first, spread_base[2]])
    table = jnp.concatenate([spread_weights, local.astype(jnp.float32)], axis=0)
    table = sort_by_plane(table, local[0])
    table = lax.all_gather(table, "gy")
    groups = count // GROUP
    width = ORDER * GROUP
    weights = table[:, : ORDER**3].reshape(halves, ORDER * ORDER, ORDER, groups, GROUP)
    weights = weights.transpose(0, 3, 1, 2, 4).reshape(halves, groups, ORDER * ORDER, width)
    cells = jnp.round(table[:, ORDER**3 :]).astype(jnp.int32).reshape(halves, 3, groups, GROUP)
    z_cell, y_cell, x_cell = cells[:, 0], cells[:, 1], cells[:, 2]
    first = jnp.min(z_cell, axis=-1)
    planes = jnp.max(z_cell, axis=-1) - first + ORDER
    z_wide = jnp.tile(z_cell, (1, 1, ORDER))[:, :, None, :]
    y_wide = jnp.tile(y_cell, (1, 1, ORDER))[:, :, None, :]
    cosine, sine = phases(x_cell, kx_index, points)
    step_cos, step_sin = phases(jnp.arange(ORDER, dtype=jnp.int32), kx_index, points)
    step_cos, step_sin = step_cos[:, None, :], step_sin[:, None, :]
    cosine, sine = cosine[:, :, None], sine[:, :, None]
    waves = jnp.concatenate(
        [cosine * step_cos - sine * step_sin, -(sine * step_cos + cosine * step_sin)], axis=-1
    ).reshape(halves, groups, width, -1)
    rows = -(-(y_local + ORDER - 1) // 8) * 8
    lanes = waves.shape[-1]
    per_group = lambda q, g, *_: (q, g, 0, 0)
    lines = pl.pallas_call(
        spread_kernel,
        grid_spec=pltpu.PrefetchScalarGridSpec(
            num_scalar_prefetch=2,
            grid=(halves, groups),
            in_specs=[
                pl.BlockSpec((None, None, ORDER * ORDER, width), per_group),
                pl.BlockSpec((None, None, 1, width), per_group),
                pl.BlockSpec((None, None, 1, width), per_group),
                pl.BlockSpec((None, None, width, lanes), per_group),
            ],
            out_specs=pl.BlockSpec((z_extent, None, rows, lanes), lambda q, g, *_: (0, q, 0, 0)),
        ),
        out_shape=jax.ShapeDtypeStruct((z_extent, halves, rows, lanes), jnp.float32),
        compiler_params=pltpu.CompilerParams(dimension_semantics=("arbitrary", "arbitrary")),
    )(first, planes, weights, z_wide, y_wide, waves)
    return lines, rows


def line_waves(cell, values, slopes, index, points):
    cosine, sine = phases(cell, index, points)
    step_cos, step_sin = phases(jnp.arange(ORDER, dtype=jnp.int32), index, points)
    found = []
    for table in (values, slopes):
        real = sum(table[c][..., None] * step_cos[c] for c in range(ORDER))
        imag = sum(table[c][..., None] * step_sin[c] for c in range(ORDER))
        found.append((cosine * real - sine * imag, cosine * imag + sine * real))
    return found


def slab_forces(lines, base, frac, z_first, y_index, x_index, points):
    z_extent, ky_local, _, kx_local = lines.shape
    shifts = jnp.arange(ORDER, dtype=jnp.int32)[:, None]
    w_z, d_z = spline_weights(frac[0])
    w_y, d_y = spline_weights(frac[1])
    w_x, d_x = spline_weights(frac[2])
    plane_w, plane_d = line_tables(base[0][None, :] - z_first + shifts, w_z, d_z, z_extent)
    (wy_re, wy_im), (dy_re, dy_im) = line_waves(base[1], w_y, d_y, y_index, points)
    (wx_re, wx_im), (dx_re, dx_im) = line_waves(base[2], w_x, d_x, x_index, points)
    join = lambda a, b: jnp.concatenate([a, b], axis=1)
    waves = jnp.stack([join(wx_re, -wx_im), join(wx_im, wx_re), join(dx_re, -dx_im), join(dx_im, dx_re)])
    count = base.shape[1]
    along = jnp.einsum(
        "mk,nk->mn",
        lines.reshape(z_extent * ky_local, 2 * kx_local),
        waves.reshape(4 * count, 2 * kx_local),
        precision=HIGH,
    ).reshape(z_extent, ky_local, 4, count)
    wy_re, wy_im, dy_re, dy_im = wy_re.T, wy_im.T, dy_re.T, dy_im.T
    plain = jnp.sum(along[:, :, 0] * wy_re - along[:, :, 1] * wy_im, axis=1)
    tilted = jnp.sum(along[:, :, 0] * dy_re - along[:, :, 1] * dy_im, axis=1)
    sloped = jnp.sum(along[:, :, 2] * wy_re - along[:, :, 3] * wy_im, axis=1)
    return jnp.stack(
        [
            jnp.sum(plain * plane_d, axis=0),
            jnp.sum(tilted * plane_w, axis=0),
            jnp.sum(sloped * plane_w, axis=0),
        ]
    )


def shards(spread_weights, spread_base, qm_base, qm_frac, qm_charge):
    points = GRID
    margin = ORDER - 1
    count_z = lax.axis_size("gz")
    count_y = lax.axis_size("gy")
    z_local = points // count_z
    y_local = points // count_y
    z_extent = z_local + margin
    kx_count = points // 2
    kx_local = kx_count // count_y
    ky_local = points // count_z
    z_first = lax.axis_index("gz") * z_local
    y_first = lax.axis_index("gy") * y_local
    ky_index = lax.axis_index("gz") * ky_local + jnp.arange(ky_local, dtype=jnp.int32)
    kx_index = lax.axis_index("gy") * kx_local + jnp.arange(kx_local, dtype=jnp.int32)
    positions = jnp.arange(points, dtype=jnp.int32)
    all_base = lax.all_gather(qm_base, ("gz", "gy"), axis=1, tiled=True)
    all_frac = lax.all_gather(qm_frac, ("gz", "gy"), axis=1, tiled=True)

    lines, rows = spread_lines(
        spread_weights, spread_base, z_first, y_first, z_extent, y_local, kx_index, points
    )
    row_cells = (
        jnp.arange(count_y, dtype=jnp.int32)[:, None] * y_local
        + jnp.arange(rows, dtype=jnp.int32)[None, :]
    ).reshape(-1) % points
    tables = jnp.concatenate(angle_tables(positions, row_cells, points), axis=0)
    lines = lines.reshape(z_extent, count_y * rows, 2 * kx_local)
    both = jnp.einsum("yr,zrk->zyk", tables, lines, precision=HIGH)
    with_cos, with_sin = both[:, :points], both[:, points:]
    packed = jnp.stack(
        [
            with_cos[:, :, :kx_local] + with_sin[:, :, kx_local:],
            with_cos[:, :, kx_local:] - with_sin[:, :, :kx_local],
        ],
        axis=1,
    )
    packed = packed.reshape(z_extent, 2, count_z, ky_local, kx_local).transpose(2, 0, 1, 3, 4)
    packed = packed.reshape(count_z, z_extent * 2 * ky_local * kx_local)
    moved = lax.all_to_all(packed, "gz", split_axis=0, concat_axis=0, tiled=True)

    z_cells = (
        jnp.arange(count_z, dtype=jnp.int32)[:, None] * z_local
        + jnp.arange(z_extent, dtype=jnp.int32)[None, :]
    ).reshape(-1) % points
    cells = ky_local * kx_local
    moved = moved.reshape(count_z * z_extent, 2 * cells)
    tables = jnp.concatenate(angle_tables(positions, z_cells, points), axis=0)
    both = jnp.dot(tables, moved, precision=HIGH).reshape(2, points, 2, ky_local, kx_local)
    green = influence(
        positions[:, None, None], ky_index[None, :, None], kx_index[None, None, :], points
    )
    kx_weight = jnp.where(kx_index == 0, 1.0, 2.0).astype(jnp.float32)
    green = green * (kx_weight * (1.0 / float(points * points * points)))
    spectrum = jnp.stack(
        [(both[0, :, 0] + both[1, :, 1]) * green, (both[0, :, 1] - both[1, :, 0]) * green], axis=1
    ).reshape(points, 2 * cells)
    back = jnp.concatenate(angle_tables(z_cells, positions, points), axis=0)
    both = jnp.dot(back, spectrum, precision=HIGH)
    both = both.reshape(2, count_z, z_extent, 2, ky_local, kx_local)
    lines = jnp.stack(
        [both[0, :, :, 0] - both[1, :, :, 1], both[0, :, :, 1] + both[1, :, :, 0]], axis=3
    )

    def one_slab(args):
        slab, base, frac, start = args
        return slab_forces(slab, base, frac, start, ky_index, kx_index, points)

    slab_base = all_base.reshape(3, count_z, -1).transpose(1, 0, 2)
    slab_frac = all_frac.reshape(3, count_z, -1).transpose(1, 0, 2)
    starts = jnp.arange(count_z, dtype=jnp.int32) * z_local
    partial = lax.map(one_slab, (lines, slab_base, slab_frac, starts))
    forces = lax.psum_scatter(
        partial.transpose(1, 0, 2).reshape(3, -1), ("gz", "gy"), scatter_dimension=1, tiled=True
    )
    return -qm_charge * forces


def solution(mesh):
    in_specs = (
        P(None, ("gz", "gy")),
        P(None, ("gz", "gy")),
        P(None, ("gz", "gy")),
        P(None, ("gz", "gy")),
        P(("gz", "gy")),
    )
    out_specs = P(None, ("gz", "gy"))
    return jax.shard_map(shards, mesh=mesh, in_specs=in_specs, out_specs=out_specs, check_vma=False)
```
